32 devices in a mesh: ctx: 8 (over y, x, core), ch: 4 (over z).
Axes of the slice: x: 2, y: 2, z: 4, core: 2. Of those that a mesh axis runs over, the one named last changes fastest.
Arguments:
- tokens_in: bfloat16 [1792, 4096], P('ctx', 'ch'), may hold values from -6 to 6
- norm_gain: bfloat16 [4096], P('ch'), may hold values from 0.5 to 1.5
- w_qkv: bfloat16 [4096, 3, 2048], P('ch'), may hold values from -0.09375 to 0.09375
- short_filter: float32 [3, 3, 2048], P(None, None, 'ch'), may hold values from -3.5 to 3.5
- residue: float32 [2048, 16], P('ch'), may hold values from -1.5 to 1.5
- decay_rate: float32 [2048, 16], P('ch'), may hold values from 0.00027901787 to 0.025
- skip_bias: float32 [2048], P('ch'), may hold values from -4 to 4
- w_out: bfloat16 [2048, 4096], P(None, 'ch'), may hold values from -0.125 to 0.125
Outputs:
- mixed_out: bfloat16 [1792, 4096], P('ctx', 'ch')
The draws below stay inside these ranges and needn't reach their ends.
All inputs are finite; a program needn't handle non-finite values.
Results may differ from the reference program's by a relative error of at most 0.011.
Values may be sent and summed in bfloat16 or wider, within the bound.
A program may use at most 128 MiB of HBM per device.

```python
import math
import jax
import jax.numpy as jnp
from jax import lax

D = 4096
SHORT = 3
ORDER = 16
TOKENS = 1792
SLAB = 2048


def level_of(own_key, dims, cuts, smallest, largest):
    loudness = 1.0
    for dim, shards_of in cuts:
        heights = jax.random.uniform(jax.random.fold_in(jax.random.fold_in(own_key, 6), dim), (shards_of,), jnp.float32, smallest / len(cuts), largest / len(cuts))
        loudness = loudness * jnp.repeat(jnp.exp(heights), dims[dim] // shards_of).reshape((-1,) + (1,) * (len(dims) - 1 - dim))
    return loudness


def normal_values(stream_key, dims, scale, most, split=(), dtype=jnp.bfloat16):
    result = scale * jax.random.normal(stream_key, dims, jnp.float32)
    if split:
        result = result * level_of(stream_key, dims, split, -0.22, 0.18)
    return jnp.clip(result, -most, most).astype(dtype)


def setup_inputs(seed: int = 0) -> dict:
    key_list = jax.random.split(jax.random.key(seed), 9)
    return {
        "tokens_in": normal_values(key_list[0], (TOKENS, D), 1.0, 6.0, ((0, 8), (1, 4))),
        "norm_gain": jnp.clip(1.0 + 0.1 * jax.random.normal(key_list[1], (D,), jnp.float32), 0.5, 1.5).astype(jnp.bfloat16),
        "w_qkv": normal_values(key_list[2], (D, 3, SLAB), D ** -0.5, 0.09375, ((0, 4),)),
        "short_filter": normal_values(key_list[3], (SHORT, 3, SLAB), SHORT ** -0.5, 3.5, ((2, 4),), jnp.float32),
        "residue": normal_values(key_list[4], (SLAB, ORDER), ORDER ** -0.5, 1.5, ((0, 4),), jnp.float32),
        "decay_rate": jnp.clip(jnp.exp(math.log(0.025) - 4.495355 * jax.random.uniform(key_list[5], (SLAB, ORDER), jnp.float32) ** level_of(key_list[5], (SLAB, ORDER), ((0, 4),), -0.2, 0.2)), 0.00027901787, 0.025),
        "skip_bias": normal_values(key_list[6], (SLAB,), 1.0, 4.0, ((0, 4),), jnp.float32),
        "w_out": normal_values(key_list[7], (SLAB, D), SLAB ** -0.5, 0.125, ((1, 4),)),
    }


def reference(tokens_in, norm_gain, w_qkv, short_filter, residue, decay_rate, skip_bias, w_out):
    total = tokens_in.shape[0]
    chans = w_qkv.shape[2]
    wide = tokens_in.astype(jnp.float32)
    scaled = (wide * norm_gain.astype(jnp.float32)).astype(jnp.bfloat16)
    mean_sq = lax.optimization_barrier(jnp.mean(wide * wide, axis=1))
    proj = jnp.dot(scaled, w_qkv.reshape(D, 3 * chans), preferred_element_type=jnp.float32).reshape(total, 3, chans)
    feats = (proj * lax.rsqrt(mean_sq + 1e-06)[:, None, None]).astype(jnp.bfloat16)
    padded = jnp.concatenate([jnp.zeros((SHORT - 1, 3, chans), jnp.bfloat16), feats], axis=0).astype(jnp.float32)
    featurized = sum((short_filter[lag_index][None] * padded[SHORT - 1 - lag_index:SHORT - 1 - lag_index + total] for lag_index in range(SHORT)))
    query = featurized[:, 0]
    gated = (featurized[:, 1] * featurized[:, 2]).astype(jnp.bfloat16)
    lag_values = lax.iota(jnp.float32, total)
    block_size = 32
    blocks = chans // block_size
    signal = gated.astype(jnp.float32).T.reshape(blocks, block_size, total)
    residues = residue.reshape(blocks, block_size, ORDER)
    decays = decay_rate.reshape(blocks, block_size, ORDER)

    def block_conv(packed):
        block_signal, block_residue, block_decay = packed
        filt = lax.optimization_barrier(jnp.sum(block_residue[:, :, None] * jnp.sqrt(2.0 * block_decay)[:, :, None] * jnp.exp(-block_decay[:, :, None] * lag_values[None, None, :]), axis=1))
        spectrum = jnp.fft.rfft(block_signal, n=2 * total) * jnp.fft.rfft(filt, n=2 * total)
        return jnp.fft.irfft(spectrum, n=2 * total)[:, :total]
    conv = lax.map(block_conv, (signal, residues, decays)).reshape(chans, total).T.astype(jnp.bfloat16)
    gated_out = (query * (conv.astype(jnp.float32) + skip_bias[None, :] * gated.astype(jnp.float32))).astype(jnp.bfloat16)
    return jnp.dot(gated_out, w_out, preferred_element_type=jnp.float32).astype(jnp.bfloat16)
```

```python
import functools

import jax
import jax.numpy as jnp
from jax import lax
from jax.experimental import pallas as pl
from jax.experimental.pallas import tpu as pltpu
from jax.sharding import PartitionSpec as P

D = 4096
SHORT = 3
ORDER = 16
LANES = 128
SUB = 32
HALO = 16
MESH = pl.DeviceIdType.MESH


def kernel(
    n_ctx, n_ch, rows, chunks,
    tok_ref, gain_ref, w_hbm, sf_ref, res_ref, dec_ref, skip_ref, wout_hbm, out_ref,
    scaled, wbuf, woutbuf, up_send, up_recv, dn_send, dn_recv,
    sq_send, sq_recv, square, scale_ref, p_sf, p_res, p_dec, p_skip,
    fpad, halo_send, halo_recv, st_send, st_recv, local_st, gz, gated_ref, query_ref, local_y, gobuf,
    w_sem, wout_sem, up_ss, up_rs, dn_ss, dn_rs, sq_ss, sq_rs, p_ss, p_rs,
    h_ss, h_rs, st_ss, st_rs, gu_ss, gu_rs, gd_ss, gd_rs,
):
    me = lax.axis_index("ctx")
    z = lax.axis_index("ch")
    last = n_ch - 1
    width = 3 * LANES
    half = chunks * LANES
    blocks = rows // SUB
    dev_ch = sf_ref.shape[2]
    is_end = (z == 0) | (z == last)

    def weight_copies(index):
        start = pl.multiple_of(index * LANES, LANES)
        return [
            pltpu.make_async_copy(
                w_hbm.at[s, :, pl.ds(start, LANES)],
                wbuf.at[index, :, pl.ds(s * LANES, LANES)],
                w_sem.at[index, s],
            )
            for s in range(3)
        ]

    def start_weights(j, _):
        for copy in weight_copies(chunks + j):
            copy.start()
        for copy in weight_copies(j):
            copy.start()
        return 0

    lax.fori_loop(0, chunks, start_weights, 0)
    wout_copy = pltpu.make_async_copy(wout_hbm, woutbuf, wout_sem)
    wout_copy.start()

    barrier = pltpu.get_barrier_semaphore()
    for k in range(1, n_ch):
        pl.semaphore_signal(
            barrier, inc=1, device_id={"ch": lax.rem(z + k, n_ch)}, device_id_type=MESH
        )

    def greet(k, _):
        pl.semaphore_signal(
            barrier, inc=1, device_id={"ctx": lax.rem(me + k, n_ctx)}, device_id_type=MESH
        )
        return 0

    lax.fori_loop(1, n_ctx, greet, 0)

    wide = tok_ref[...].astype(jnp.float32)
    scaled[...] = (wide * gain_ref[...].astype(jnp.float32)).astype(jnp.bfloat16)
    wide = wide * wide
    folded = wide[:, :LANES]
    for k in range(1, wide.shape[1] // LANES):
        folded = folded + wide[:, k * LANES : (k + 1) * LANES]
    square[...] = jnp.zeros_like(square)
    square[pl.ds(0, rows), :] = folded
    turned = jnp.sum(square[...].T, axis=0, keepdims=True)
    sq_send[...] = jnp.broadcast_to(turned, sq_send.shape)

    pl.semaphore_wait(barrier, n_ch - 1 + n_ctx - 1)

    def sq_copy(k):
        return pltpu.make_async_remote_copy(
            src_ref=sq_send, dst_ref=sq_recv.at[k - 1], send_sem=sq_ss.at[k - 1],
            recv_sem=sq_rs.at[k - 1], device_id={"ch": lax.rem(z + k, n_ch)}, device_id_type=MESH,
        )

    for k in range(1, n_ch):
        sq_copy(k).start()
    own_half = lax.rem(z, 2)
    partner = z + 1 - 2 * own_half
    p_copies = [
        pltpu.make_async_remote_copy(
            src_ref=src, dst_ref=dst.at[own_half], send_sem=p_ss.at[i], recv_sem=p_rs.at[i],
            device_id={"ch": partner}, device_id_type=MESH,
        )
        for i, (src, dst) in enumerate(
            ((sf_ref, p_sf), (res_ref, p_res), (dec_ref, p_dec), (skip_ref, p_skip))
        )
    ]
    for copy in p_copies:
        copy.start()
    p_sf[own_half] = sf_ref[...]
    p_res[own_half] = res_ref[...]
    p_dec[own_half] = dec_ref[...]
    p_skip[own_half] = skip_ref[...]

    def partial(index):
        for copy in weight_copies(index):
            copy.wait()
        return jnp.dot(scaled[...], wbuf[index], preferred_element_type=jnp.float32)

    def up_copy(j):
        return pltpu.make_async_remote_copy(
            src_ref=up_send.at[j], dst_ref=up_recv.at[j], send_sem=up_ss.at[j],
            recv_sem=up_rs.at[j], device_id={"ch": jnp.minimum(z + 1, last)}, device_id_type=MESH,
        )

    def dn_copy(j):
        return pltpu.make_async_remote_copy(
            src_ref=dn_send.at[j], dst_ref=dn_recv.at[j], send_sem=dn_ss.at[j],
            recv_sem=dn_rs.at[j], device_id={"ch": jnp.maximum(z - 1, 0)}, device_id_type=MESH,
        )

    def halo_copy(j):
        return pltpu.make_async_remote_copy(
            src_ref=halo_send.at[j], dst_ref=halo_recv.at[j], send_sem=h_ss.at[j],
            recv_sem=h_rs.at[j], device_id={"ctx": jnp.minimum(me + 1, n_ctx - 1)}, device_id_type=MESH,
        )

    def state_copy(j, k):
        return pltpu.make_async_remote_copy(
            src_ref=st_send.at[j], dst_ref=st_recv.at[j, k - 1], send_sem=st_ss.at[j],
            recv_sem=st_rs.at[j], device_id={"ctx": lax.rem(me + k, n_ctx)}, device_id_type=MESH,
        )

    def gu_copy(j):
        piece = gobuf.at[:, pl.ds(pl.multiple_of(j * LANES, LANES), LANES)]
        return pltpu.make_async_remote_copy(
            src_ref=piece, dst_ref=piece, send_sem=gu_ss.at[j],
            recv_sem=gu_rs.at[j], device_id={"ch": jnp.minimum(z + 1, last)}, device_id_type=MESH,
        )

    def gd_copy(j):
        piece = gobuf.at[:, pl.ds(pl.multiple_of(half + j * LANES, LANES), LANES)]
        return pltpu.make_async_remote_copy(
            src_ref=piece, dst_ref=piece, send_sem=gd_ss.at[j],
            recv_sem=gd_rs.at[j], device_id={"ch": jnp.maximum(z - 1, 0)}, device_id_type=MESH,
        )

    def finish_scale():
        total = sq_send[...]
        for k in range(1, n_ch):
            total = total + sq_recv[k - 1]
        mean_sq = jnp.broadcast_to(total[0:1] * (1.0 / D), (LANES, total.shape[1])).T
        scale_ref[...] = lax.rsqrt(mean_sq + 1e-06)[:rows]

    def stage_a(j, proj):
        scale = scale_ref[...]
        for s in range(3):
            feats = (proj[:, s * LANES : (s + 1) * LANES] * scale).astype(jnp.bfloat16)
            fpad[j, s, pl.ds(HALO, rows), :] = feats.astype(jnp.float32)
            halo_send[j, s] = feats[rows - HALO :]

        @pl.when(me < n_ctx - 1)
        def _():
            halo_copy(j).start()

    def lane_of(j):
        per = dev_ch // LANES
        return j // per, pl.ds(pl.multiple_of(lax.rem(j, per) * LANES, LANES), LANES)

    def stage_b(j):
        side, lanes = lane_of(j)

        @pl.when(me > 0)
        def _():
            halo_copy(j).wait_recv()
            for s in range(3):
                fpad[j, s, pl.ds(0, HALO), :] = halo_recv[j, s].astype(jnp.float32)

        @pl.when(me == 0)
        def _():
            for s in range(3):
                fpad[j, s, pl.ds(0, HALO), :] = jnp.zeros((HALO, LANES), jnp.float32)

        def featurized(s):
            total = p_sf[side, 0, pl.ds(s, 1), lanes] * fpad[j, s, pl.ds(HALO, rows), :]
            for lag in range(1, SHORT):
                tap = p_sf[side, lag, pl.ds(s, 1), lanes]
                total = total + tap * fpad[j, s, pl.ds(HALO - lag, rows), :]
            return total

        query_ref[j] = featurized(0)
        gated = (featurized(1) * featurized(2)).astype(jnp.bfloat16).astype(jnp.float32)
        gated_ref[j] = gated
        for b in range(blocks):
            gz[b, pl.ds(SUB, SUB), :] = gated[b * SUB : (b + 1) * SUB]
        decay = p_dec[side, :, lanes]
        weight = p_res[side, :, lanes] * jnp.sqrt(2.0 * decay)
        lag_rows = lax.broadcasted_iota(jnp.int32, (SUB, LANES), 0).astype(jnp.float32)
        taps = jnp.zeros((SUB, LANES), jnp.float32)
        for r in range(ORDER):
            taps = taps + weight[r : r + 1] * jnp.exp(-decay[r : r + 1] * lag_rows)
        falls = [jnp.exp(decay * (-float(SUB - 1 - u))) for u in range(SUB)]
        jump = jnp.exp(decay * (-float(SUB)))

        def block(b, state):
            local_st[j, b] = state
            total = taps[0:1] * gz[b, pl.ds(SUB, SUB), :]
            for k in range(1, SUB):
                total = total + taps[k : k + 1] * gz[b, pl.ds(SUB - k, SUB), :]
            local_y[j, b] = total
            state = state * jump
            for u in range(SUB):
                state = state + falls[u] * gz[b, pl.ds(SUB + u, 1), :]
            return state

        state = lax.fori_loop(0, blocks, block, jnp.zeros((ORDER, LANES), jnp.float32))
        st_send[j] = state

        def send(k, _):
            state_copy(j, k).start()
            return 0

        lax.fori_loop(1, n_ctx, send, 0)

    def stage_c(j):
        side, lanes = lane_of(j)
        pltpu.make_async_copy(st_recv.at[j], st_recv.at[j], st_rs.at[j]).wait()
        decay = p_dec[side, :, lanes]
        weight = p_res[side, :, lanes] * jnp.sqrt(2.0 * decay)

        def gather(k, state):
            far = jnp.full((ORDER, LANES), (k - 1) * rows, jnp.int32).astype(jnp.float32)
            term = jnp.exp(-decay * far) * st_recv[j, k - 1]
            return state + jnp.where(jnp.full((ORDER, LANES), k, jnp.int32) <= me, term, 0.0)

        incoming = lax.fori_loop(1, n_ctx, gather, jnp.zeros((ORDER, LANES), jnp.float32))
        lag_rows = lax.broadcasted_iota(jnp.int32, (SUB, LANES), 0).astype(jnp.float32) + 1.0
        tables = [
            weight[r : r + 1] * jnp.exp(-decay[r : r + 1] * lag_rows) for r in range(ORDER)
        ]
        jump = jnp.exp(decay * (-float(SUB)))
        skip = p_skip[side, :, lanes]
        start = pl.multiple_of(jnp.where(z == 0, 0, half) + j * LANES, LANES)
        for b in range(blocks):
            state = local_st[j, b] + incoming
            total = local_y[j, b]
            for r in range(ORDER):
                total = total + tables[r] * state[r : r + 1]
            conv = total.astype(jnp.bfloat16).astype(jnp.float32)
            span = pl.ds(b * SUB, SUB)
            mixed = query_ref[j, span, :] * (conv + skip * gated_ref[j, span, :])
            gobuf[span, pl.ds(start, LANES)] = mixed.astype(jnp.bfloat16)
            incoming = incoming * jump

        @pl.when(z == 0)
        def _():
            gu_copy(j).start()

        @pl.when(z == last)
        def _():
            gd_copy(j).start()

    gz[...] = jnp.zeros_like(gz)

    def step(s, _):
        cu = s - z
        cd = s - (last - z)
        fin = s - last

        @pl.when((z < last) & (cu >= 0) & (cu < chunks))
        def _():
            total = partial(chunks + cu)

            @pl.when(z == 0)
            def _():
                up_send[cu] = total.astype(jnp.bfloat16)

            @pl.when(z > 0)
            def _():
                up_copy(cu).wait_recv()
                up_send[cu] = (total + up_recv[cu].astype(jnp.float32)).astype(jnp.bfloat16)

            up_copy(cu).start()

        @pl.when((z > 0) & (cd >= 0) & (cd < chunks))
        def _():
            total = partial(cd)

            @pl.when(z == last)
            def _():
                dn_send[cd] = total.astype(jnp.bfloat16)

            @pl.when(z < last)
            def _():
                dn_copy(cd).wait_recv()
                dn_send[cd] = (total + dn_recv[cd].astype(jnp.float32)).astype(jnp.bfloat16)

            dn_copy(cd).start()

        @pl.when(s == last)
        def _():
            for k in range(1, n_ch):
                sq_copy(k).wait()
            for copy in p_copies:
                copy.wait()
            finish_scale()

        @pl.when(is_end & (fin >= 2) & (fin < chunks + 2))
        def _():
            stage_c(fin - 2)

        @pl.when(is_end & (fin >= 1) & (fin < chunks + 1))
        def _():
            stage_b(fin - 1)

        @pl.when((z == 0) & (fin >= 0) & (fin < chunks))
        def _():
            total = partial(fin)
            dn_copy(fin).wait_recv()
            stage_a(fin, total + dn_recv[fin].astype(jnp.float32))

        @pl.when((z == last) & (fin >= 0) & (fin < chunks))
        def _():
            total = partial(chunks + fin)
            up_copy(fin).wait_recv()
            stage_a(fin, total + up_recv[fin].astype(jnp.float32))

        fu = s - (last + 2) - 2 * z
        fd = s - (last + 2) - 2 * (last - z)

        @pl.when((z > 0) & (z < last) & (fu >= 0) & (fu < chunks))
        def _():
            gu_copy(fu).wait_recv()
            gu_copy(fu).start()

        @pl.when((z > 0) & (z < last) & (fd >= 0) & (fd < chunks))
        def _():
            gd_copy(fd).wait_recv()
            gd_copy(fd).start()

        return 0

    lax.fori_loop(0, chunks + last + 2 + 2 * (last - 1), step, 0)

    wout_copy.wait()

    def finish(j, _):
        @pl.when(z < last)
        def _():
            up_copy(j).wait_send()
            gu_copy(j).wait_send()

        @pl.when(z > 0)
        def _():
            dn_copy(j).wait_send()
            gd_copy(j).wait_send()

        @pl.when(z == last)
        def _():
            gu_copy(j).wait_recv()

        @pl.when(z == 0)
        def _():
            gd_copy(j).wait_recv()

        @pl.when(is_end & (me < n_ctx - 1))
        def _():
            halo_copy(j).wait_send()

        @pl.when(is_end)
        def _():
            pltpu.make_async_copy(st_recv.at[j], st_recv.at[j], st_ss.at[j]).wait()

        return 0

    lax.fori_loop(0, chunks, finish, 0)

    tile = 256

    def project(t, _):
        cols = pl.ds(pl.multiple_of(t * tile, tile), tile)
        out_ref[:, cols] = jnp.dot(
            gobuf[...], woutbuf[:, cols], preferred_element_type=jnp.float32
        ).astype(jnp.bfloat16)
        return 0

    lax.fori_loop(0, out_ref.shape[1] // tile, project, 0)


def local(tokens_in, norm_gain, w_qkv, short_filter, residue, decay_rate, skip_bias, w_out):
    rows, feat = tokens_in.shape
    slab = w_qkv.shape[2]
    dev_ch = short_filter.shape[2]
    n_ctx = lax.axis_size("ctx")
    n_ch = lax.axis_size("ch")
    chunks = slab // 2 // LANES
    width = 3 * LANES
    padded = -(-rows // LANES) * LANES
    blocks = rows // SUB
    vmem = pl.BlockSpec(memory_space=pltpu.VMEM)
    hbm = pl.BlockSpec(memory_space=pl.ANY)
    bf, f32 = jnp.bfloat16, jnp.float32
    dma = pltpu.SemaphoreType.DMA
    V = pltpu.VMEM
    return pl.pallas_call(
        functools.partial(kernel, n_ctx, n_ch, rows, chunks),
        out_shape=jax.ShapeDtypeStruct((rows, w_out.shape[1]), bf),
        in_specs=[vmem, vmem, hbm, vmem, vmem, vmem, vmem, hbm],
        out_specs=vmem,
        scratch_shapes=[
            V((rows, feat), bf), V((2 * chunks, feat, width), bf), V(w_out.shape, bf),
            V((chunks, rows, width), bf), V((chunks, rows, width), bf),
            V((chunks, rows, width), bf), V((chunks, rows, width), bf),
            V((8, padded), f32), V((n_ch - 1, 8, padded), f32), V((padded, LANES), f32),
            V((rows, LANES), f32),
            V((2, SHORT, 3, dev_ch), f32), V((2, ORDER, dev_ch), f32), V((2, ORDER, dev_ch), f32),
            V((2, 1, dev_ch), f32),
            V((chunks, 3, HALO + rows, LANES), f32),
            V((chunks, 3, HALO, LANES), bf), V((chunks, 3, HALO, LANES), bf),
            V((chunks, ORDER, LANES), f32), V((chunks, n_ctx - 1, ORDER, LANES), f32),
            V((chunks, blocks, ORDER, LANES), f32), V((blocks, 2 * SUB, LANES), f32),
            V((chunks, rows, LANES), f32), V((chunks, rows, LANES), f32),
            V((chunks, blocks, SUB, LANES), f32), V((rows, slab), bf),
            dma((2 * chunks, 3)), dma, dma((chunks,)), dma((chunks,)), dma((chunks,)), dma((chunks,)),
            dma((n_ch - 1,)), dma((n_ch - 1,)), dma((4,)), dma((4,)),
            dma((chunks,)), dma((chunks,)), dma((chunks,)), dma((chunks,)),
            dma((chunks,)), dma((chunks,)), dma((chunks,)), dma((chunks,)),
        ],
        compiler_params=pltpu.CompilerParams(
            collective_id=0, has_side_effects=True, vmem_limit_bytes=56 * 2**20
        ),
        name="hyena",
    )(
        tokens_in, norm_gain.reshape(1, feat), jnp.transpose(w_qkv, (1, 0, 2)), short_filter,
        residue.T, decay_rate.T, skip_bias.reshape(1, dev_ch), w_out,
    )


def solution(mesh):
    return jax.shard_map(
        local,
        mesh=mesh,
        in_specs=(
            P("ctx", "ch"),
            P("ch"),
            P("ch", None, None),
            P(None, None, "ch"),
            P("ch", None),
            P("ch", None),
            P("ch"),
            P(None, "ch"),
        ),
        out_specs=P("ctx", "ch"),
        check_vma=False,
    )
```

```python
import functools

import jax
import jax.numpy as jnp
from jax import lax
from jax.experimental import pallas as pl
from jax.experimental.pallas import tpu as pltpu
from jax.sharding import PartitionSpec as P

D = 4096
SHORT = 3
ORDER = 16
LANES = 128
SUB = 32
LEAD = 8
PIECES = 2
HALO = 16
MESH = pl.DeviceIdType.MESH


def kernel(
    n_ctx, n_ch, rows, chunks,
    tok_ref, gain_ref, w_hbm, sf_ref, res_ref, dec_ref, skip_ref, wout_hbm, out_ref,
    scaled, wbuf, woutbuf, up_send, up_recv, dn_send, dn_recv,
    sq_send, sq_recv, square, scale_ref, p_sf, p_res, p_dec, p_skip,
    fpad, halo_send, halo_recv, st_send, st_recv, local_st, gz, gated_ref, query_ref, local_y, gobuf,
    w_sem, wout_sem, up_ss, up_rs, dn_ss, dn_rs, sq_ss, sq_rs, p_ss, p_rs,
    h_ss, h_rs, st_ss, st_rs, gu_ss, gu_rs, gd_ss, gd_rs,
):
    me = lax.axis_index("ctx")
    z = lax.axis_index("ch")
    last = n_ch - 1
    width = 3 * LANES
    half = chunks * LANES
    piece_rows = rows // PIECES
    blocks = rows // SUB
    dev_ch = sf_ref.shape[2]
    is_end = (z == 0) | (z == last)
    is_mid = (z > 0) & (z < last)

    def weight_copies(index):
        start = pl.multiple_of(index * LANES, LANES)
        return [
            pltpu.make_async_copy(
                w_hbm.at[s, :, pl.ds(start, LANES)],
                wbuf.at[index, :, pl.ds(s * LANES, LANES)],
                w_sem.at[index, s],
            )
            for s in range(3)
        ]

    def start_weights(j, _):
        for copy in weight_copies(chunks + j):
            copy.start()
        for copy in weight_copies(j):
            copy.start()
        return 0

    lax.fori_loop(0, chunks, start_weights, 0)
    wout_copy = pltpu.make_async_copy(wout_hbm, woutbuf, wout_sem)
    wout_copy.start()

    barrier = pltpu.get_barrier_semaphore()
    for k in range(1, n_ch):
        pl.semaphore_signal(
            barrier, inc=1, device_id={"ch": lax.rem(z + k, n_ch)}, device_id_type=MESH
        )

    def greet(k, _):
        pl.semaphore_signal(
            barrier, inc=1, device_id={"ctx": lax.rem(me + k, n_ctx)}, device_id_type=MESH
        )
        return 0

    lax.fori_loop(1, n_ctx, greet, 0)

    wide = tok_ref[...].astype(jnp.float32)
    scaled[...] = (wide * gain_ref[...].astype(jnp.float32).reshape(1, -1)).astype(jnp.bfloat16)
    wide = wide * wide
    folded = wide[:, :LANES]
    for k in range(1, wide.shape[1] // LANES):
        folded = folded + wide[:, k * LANES : (k + 1) * LANES]
    square[...] = jnp.zeros_like(square)
    square[pl.ds(0, rows), :] = folded
    turned = jnp.sum(square[...].T, axis=0, keepdims=True)
    sq_send[...] = jnp.broadcast_to(turned, sq_send.shape)

    pl.semaphore_wait(barrier, n_ch - 1 + n_ctx - 1)

    def sq_copy(k):
        return pltpu.make_async_remote_copy(
            src_ref=sq_send, dst_ref=sq_recv.at[k - 1], send_sem=sq_ss.at[k - 1],
            recv_sem=sq_rs.at[k - 1], device_id={"ch": lax.rem(z + k, n_ch)}, device_id_type=MESH,
        )

    for k in range(1, n_ch):
        sq_copy(k).start()
    own_half = lax.rem(z, 2)
    partner = z + 1 - 2 * own_half
    p_copies = [
        pltpu.make_async_remote_copy(
            src_ref=src, dst_ref=dst.at[own_half], send_sem=p_ss.at[i], recv_sem=p_rs.at[i],
            device_id={"ch": partner}, device_id_type=MESH,
        )
        for i, (src, dst) in enumerate(
            ((sf_ref, p_sf), (res_ref, p_res), (dec_ref, p_dec), (skip_ref, p_skip))
        )
    ]
    for copy in p_copies:
        copy.start()
    p_sf[own_half] = sf_ref[...]
    p_res[own_half] = res_ref[...]
    p_dec[own_half] = dec_ref[...]
    p_skip[own_half] = skip_ref[...]

    def partial(index):
        for copy in weight_copies(index):
            copy.wait()
        return jnp.dot(scaled[...], wbuf[index], preferred_element_type=jnp.float32)

    def up_copy(j, i):
        span = pl.ds(i * piece_rows, piece_rows)
        return pltpu.make_async_remote_copy(
            src_ref=up_send.at[j, span], dst_ref=up_recv.at[j, span], send_sem=up_ss.at[j, i],
            recv_sem=up_rs.at[j, i], device_id={"ch": jnp.minimum(z + 1, last)}, device_id_type=MESH,
        )

    def dn_copy(j, i):
        span = pl.ds(i * piece_rows, piece_rows)
        return pltpu.make_async_remote_copy(
            src_ref=dn_send.at[j, span], dst_ref=dn_recv.at[j, span], send_sem=dn_ss.at[j, i],
            recv_sem=dn_rs.at[j, i], device_id={"ch": jnp.maximum(z - 1, 0)}, device_id_type=MESH,
        )

    def halo_copy(j):
        return pltpu.make_async_remote_copy(
            src_ref=halo_send.at[j], dst_ref=halo_recv.at[j], send_sem=h_ss.at[j],
            recv_sem=h_rs.at[j], device_id={"ctx": jnp.minimum(me + 1, n_ctx - 1)}, device_id_type=MESH,
        )

    def state_copy(j, k):
        return pltpu.make_async_remote_copy(
            src_ref=st_send.at[j], dst_ref=st_recv.at[j, k - 1], send_sem=st_ss.at[j],
            recv_sem=st_rs.at[j], device_id={"ctx": lax.rem(me + k, n_ctx)}, device_id_type=MESH,
        )

    def gu_copy(j):
        piece = gobuf.at[:, pl.ds(pl.multiple_of(j * LANES, LANES), LANES)]
        return pltpu.make_async_remote_copy(
            src_ref=piece, dst_ref=piece, send_sem=gu_ss.at[j],
            recv_sem=gu_rs.at[j], device_id={"ch": jnp.minimum(z + 1, last)}, device_id_type=MESH,
        )

    def gd_copy(j):
        piece = gobuf.at[:, pl.ds(pl.multiple_of(half + j * LANES, LANES), LANES)]
        return pltpu.make_async_remote_copy(
            src_ref=piece, dst_ref=piece, send_sem=gd_ss.at[j],
            recv_sem=gd_rs.at[j], device_id={"ch": jnp.maximum(z - 1, 0)}, device_id_type=MESH,
        )

    def finish_scale():
        total = sq_send[...]
        for k in range(1, n_ch):
            total = total + sq_recv[k - 1]
        mean_sq = jnp.broadcast_to(total[0:1] * (1.0 / D), (LANES, total.shape[1])).T
        scale_ref[...] = lax.rsqrt(mean_sq + 1e-06)[:rows]

    def stage_a(j, proj):
        scale = scale_ref[...]
        for s in range(3):
            feats = (proj[:, s * LANES : (s + 1) * LANES] * scale).astype(jnp.bfloat16)
            fpad[j, s, pl.ds(HALO, rows), :] = feats.astype(jnp.float32)
            halo_send[j, s] = feats[rows - HALO :]

        @pl.when(me < n_ctx - 1)
        def _():
            halo_copy(j).start()

    def lane_of(j):
        per = dev_ch // LANES
        return j // per, pl.ds(pl.multiple_of(lax.rem(j, per) * LANES, LANES), LANES)

    def stage_b(j):
        side, lanes = lane_of(j)

        @pl.when(me > 0)
        def _():
            halo_copy(j).wait_recv()
            for s in range(3):
                fpad[j, s, pl.ds(0, HALO), :] = halo_recv[j, s].astype(jnp.float32)

        @pl.when(me == 0)
        def _():
            for s in range(3):
                fpad[j, s, pl.ds(0, HALO), :] = jnp.zeros((HALO, LANES), jnp.float32)

        def featurized(s):
            total = p_sf[side, 0, pl.ds(s, 1), lanes] * fpad[j, s, pl.ds(HALO, rows), :]
            for lag in range(1, SHORT):
                tap = p_sf[side, lag, pl.ds(s, 1), lanes]
                total = total + tap * fpad[j, s, pl.ds(HALO - lag, rows), :]
            return total

        query_ref[j] = featurized(0)
        gated = (featurized(1) * featurized(2)).astype(jnp.bfloat16).astype(jnp.float32)
        gated_ref[j] = gated
        for b in range(blocks):
            gz[b, pl.ds(SUB, SUB), :] = gated[b * SUB : (b + 1) * SUB]
        decay = p_dec[side, :, lanes]
        weight = p_res[side, :, lanes] * jnp.sqrt(2.0 * decay)
        lag_rows = lax.broadcasted_iota(jnp.int32, (SUB, LANES), 0).astype(jnp.float32)
        taps = jnp.zeros((SUB, LANES), jnp.float32)
        for r in range(ORDER):
            taps = taps + weight[r : r + 1] * jnp.exp(-decay[r : r + 1] * lag_rows)
        falls = [jnp.exp(decay * (-float(SUB - 1 - u))) for u in range(SUB)]
        jump = jnp.exp(decay * (-float(SUB)))

        def block(b, state):
            local_st[j, b] = state
            total = taps[0:1] * gz[b, pl.ds(SUB, SUB), :]
            for k in range(1, SUB):
                total = total + taps[k : k + 1] * gz[b, pl.ds(SUB - k, SUB), :]
            local_y[j, b] = total
            state = state * jump
            for u in range(SUB):
                state = state + falls[u] * gz[b, pl.ds(SUB + u, 1), :]
            return state

        state = lax.fori_loop(0, blocks, block, jnp.zeros((ORDER, LANES), jnp.float32))
        st_send[j // 2, lax.rem(j, 2)] = state

        def send(k, _):
            state_copy(j // 2, k).start()
            return 0

        @pl.when(lax.rem(j, 2) == 1)
        def _():
            lax.fori_loop(1, n_ctx, send, 0)

    def stage_c(j):
        side, lanes = lane_of(j)
        pair = j // 2

        @pl.when(lax.rem(j, 2) == 0)
        def _():
            pltpu.make_async_copy(st_recv.at[pair], st_recv.at[pair], st_rs.at[pair]).wait()

        decay = p_dec[side, :, lanes]
        weight = p_res[side, :, lanes] * jnp.sqrt(2.0 * decay)

        def gather(k, state):
            far = jnp.full((ORDER, LANES), (k - 1) * rows, jnp.int32).astype(jnp.float32)
            term = jnp.exp(-decay * far) * st_recv[pair, k - 1, lax.rem(j, 2)]
            return state + jnp.where(jnp.full((ORDER, LANES), k, jnp.int32) <= me, term, 0.0)

        incoming = lax.fori_loop(1, n_ctx, gather, jnp.zeros((ORDER, LANES), jnp.float32))
        lag_rows = lax.broadcasted_iota(jnp.int32, (SUB, LANES), 0).astype(jnp.float32) + 1.0
        tables = [
            weight[r : r + 1] * jnp.exp(-decay[r : r + 1] * lag_rows) for r in range(ORDER)
        ]
        jump = jnp.exp(decay * (-float(SUB)))
        skip = p_skip[side, :, lanes]
        start = pl.multiple_of(jnp.where(z == 0, 0, half) + j * LANES, LANES)
        for b in range(blocks):
            state = local_st[j, b] + incoming
            total = local_y[j, b]
            for r in range(ORDER):
                total = total + tables[r] * state[r : r + 1]
            conv = total.astype(jnp.bfloat16).astype(jnp.float32)
            span = pl.ds(b * SUB, SUB)
            mixed = query_ref[j, span, :] * (conv + skip * gated_ref[j, span, :])
            gobuf[span, pl.ds(start, LANES)] = mixed.astype(jnp.bfloat16)
            incoming = incoming * jump

        @pl.when(z == 0)
        def _():
            gu_copy(j).start()

        @pl.when(z == last)
        def _():
            gd_copy(j).start()

    def lead_up(j, _):
        up_send[j] = partial(chunks + j).astype(jnp.bfloat16)
        for i in range(PIECES):
            up_copy(j, i).start()
        return 0

    def lead_dn(j, _):
        dn_send[j] = partial(j).astype(jnp.bfloat16)
        for i in range(PIECES):
            dn_copy(j, i).start()
        return 0

    @pl.when(z == 0)
    def _():
        lax.fori_loop(0, LEAD, lead_up, 0)

    @pl.when(z == last)
    def _():
        lax.fori_loop(0, LEAD, lead_dn, 0)

    gz[...] = jnp.zeros_like(gz)
    def settle():
        for k in range(1, n_ch):
            sq_copy(k).wait()
        for copy in p_copies:
            copy.wait()

    @pl.when(is_end)
    def _():
        settle()
        finish_scale()

    def step(s, _):
        cu = s + 1 - z
        cd = s + 1 - (last - z)
        fin = s

        @pl.when((z == 0) & (s + LEAD < chunks))
        def _():
            lead_up(s + LEAD, 0)

        @pl.when((z == last) & (s + LEAD < chunks))
        def _():
            lead_dn(s + LEAD, 0)

        @pl.when(is_mid & (cu >= 0) & (cu < chunks))
        def _():
            total = partial(chunks + cu)
            for i in range(PIECES):
                span = pl.ds(i * piece_rows, piece_rows)
                up_copy(cu, i).wait_recv()
                mine = total[i * piece_rows : (i + 1) * piece_rows]
                theirs = up_recv[cu, span, :].astype(jnp.float32)
                up_send[cu, span, :] = (mine + theirs).astype(jnp.bfloat16)
                up_copy(cu, i).start()

        @pl.when(is_mid & (cd >= 0) & (cd < chunks))
        def _():
            total = partial(cd)
            for i in range(PIECES):
                span = pl.ds(i * piece_rows, piece_rows)
                dn_copy(cd, i).wait_recv()
                mine = total[i * piece_rows : (i + 1) * piece_rows]
                theirs = dn_recv[cd, span, :].astype(jnp.float32)
                dn_send[cd, span, :] = (mine + theirs).astype(jnp.bfloat16)
                dn_copy(cd, i).start()

        @pl.when(is_end & (fin >= 3) & (fin < chunks + 3))
        def _():
            stage_c(fin - 3)

        @pl.when(is_end & (fin >= 1) & (fin < chunks + 1))
        def _():
            stage_b(fin - 1)

        @pl.when((z == 0) & (fin >= 0) & (fin < chunks))
        def _():
            total = partial(fin)
            for i in range(PIECES):
                dn_copy(fin, i).wait_recv()
            stage_a(fin, total + dn_recv[fin].astype(jnp.float32))

        @pl.when((z == last) & (fin >= 0) & (fin < chunks))
        def _():
            total = partial(chunks + fin)
            for i in range(PIECES):
                up_copy(fin, i).wait_recv()
            stage_a(fin, total + up_recv[fin].astype(jnp.float32))

        fu = s - chunks + 3 - 2 * z
        fd = s - chunks + 3 - 2 * (last - z)

        @pl.when((z > 0) & (z < last) & (fu >= 0) & (fu < chunks))
        def _():
            gu_copy(fu).wait_recv()
            gu_copy(fu).start()

        @pl.when((z > 0) & (z < last) & (fd >= 0) & (fd < chunks))
        def _():
            gd_copy(fd).wait_recv()
            gd_copy(fd).start()

        return 0

    lax.fori_loop(0, 2 * chunks - 3 + 2 * (last - 1), step, 0)

    @pl.when(is_mid)
    def _():
        settle()

    wout_copy.wait()

    def finish(j, _):
        @pl.when(z < last)
        def _():
            for i in range(PIECES):
                up_copy(j, i).wait_send()
            gu_copy(j).wait_send()

        @pl.when(z > 0)
        def _():
            for i in range(PIECES):
                dn_copy(j, i).wait_send()
            gd_copy(j).wait_send()

        @pl.when(z == last)
        def _():
            gu_copy(j).wait_recv()

        @pl.when(z == 0)
        def _():
            gd_copy(j).wait_recv()

        @pl.when(is_end & (me < n_ctx - 1))
        def _():
            halo_copy(j).wait_send()

        @pl.when(is_end & (j < chunks // 2))
        def _():
            pltpu.make_async_copy(st_recv.at[j], st_recv.at[j], st_ss.at[j]).wait()

        return 0

    lax.fori_loop(0, chunks, finish, 0)

    tile = 256

    def project(t, _):
        cols = pl.ds(pl.multiple_of(t * tile, tile), tile)
        out_ref[:, cols] = jnp.dot(
            gobuf[...], woutbuf[:, cols], preferred_element_type=jnp.float32
        ).astype(jnp.bfloat16)
        return 0

    lax.fori_loop(0, out_ref.shape[1] // tile, project, 0)


def local(tokens_in, norm_gain, w_qkv, short_filter, residue, decay_rate, skip_bias, w_out):
    rows, feat = tokens_in.shape
    slab = w_qkv.shape[2]
    dev_ch = short_filter.shape[2]
    n_ctx = lax.axis_size("ctx")
    n_ch = lax.axis_size("ch")
    chunks = slab // 2 // LANES
    width = 3 * LANES
    padded = -(-rows // LANES) * LANES
    blocks = rows // SUB
    vmem = pl.BlockSpec(memory_space=pltpu.VMEM)
    hbm = pl.BlockSpec(memory_space=pl.ANY)
    bf, f32 = jnp.bfloat16, jnp.float32
    dma = pltpu.SemaphoreType.DMA
    V = pltpu.VMEM
    return pl.pallas_call(
        functools.partial(kernel, n_ctx, n_ch, rows, chunks),
        out_shape=jax.ShapeDtypeStruct((rows, w_out.shape[1]), bf),
        in_specs=[vmem, vmem, hbm, vmem, vmem, vmem, vmem, hbm],
        out_specs=vmem,
        scratch_shapes=[
            V((rows, feat), bf), V((2 * chunks, feat, width), bf), V(w_out.shape, bf),
            V((chunks, rows, width), bf), V((chunks, rows, width), bf),
            V((chunks, rows, width), bf), V((chunks, rows, width), bf),
            V((8, padded), f32), V((n_ch - 1, 8, padded), f32), V((padded, LANES), f32),
            V((rows, LANES), f32),
            V((2, SHORT, 3, dev_ch), f32), V((2, ORDER, dev_ch), f32), V((2, ORDER, dev_ch), f32),
            V((2, 1, dev_ch), f32),
            V((chunks, 3, HALO + rows, LANES), f32),
            V((chunks, 3, HALO, LANES), bf), V((chunks, 3, HALO, LANES), bf),
            V((chunks // 2, 2, ORDER, LANES), f32), V((chunks // 2, n_ctx - 1, 2, ORDER, LANES), f32),
            V((chunks, blocks, ORDER, LANES), f32), V((blocks, 2 * SUB, LANES), f32),
            V((chunks, rows, LANES), f32), V((chunks, rows, LANES), f32),
            V((chunks, blocks, SUB, LANES), f32), V((rows, slab), bf),
            dma((2 * chunks, 3)), dma, dma((chunks, PIECES)), dma((chunks, PIECES)),
            dma((chunks, PIECES)), dma((chunks, PIECES)),
            dma((n_ch - 1,)), dma((n_ch - 1,)), dma((4,)), dma((4,)),
            dma((chunks,)), dma((chunks,)), dma((chunks // 2,)), dma((chunks // 2,)),
            dma((chunks,)), dma((chunks,)), dma((chunks,)), dma((chunks,)),
        ],
        compiler_params=pltpu.CompilerParams(
            collective_id=0, has_side_effects=True, vmem_limit_bytes=56 * 2**20
        ),
        name="hyena",
    )(
        tokens_in, norm_gain, jnp.transpose(w_qkv, (1, 0, 2)), short_filter,
        residue.T, decay_rate.T, skip_bias.reshape(1, dev_ch), w_out,
    )


def solution(mesh):
    return jax.shard_map(
        local,
        mesh=mesh,
        in_specs=(
            P("ctx", "ch"),
            P("ch"),
            P("ch", None, None),
            P(None, None, "ch"),
            P("ch", None),
            P("ch", None),
            P("ch"),
            P(None, "ch"),
        ),
        out_specs=P("ctx", "ch"),
        check_vma=False,
    )
```

```python
import functools

import jax
import jax.numpy as jnp
from jax import lax
from jax.experimental import pallas as pl
from jax.experimental.pallas import tpu as pltpu
from jax.sharding import PartitionSpec as P

D = 4096
SHORT = 3
ORDER = 16
LANES = 128
SUB = 32
LEAD = 8
PIECES = 2
HALO = 16
MESH = pl.DeviceIdType.MESH


def kernel(
    n_ctx, n_ch, rows, chunks,
    tok_ref, gain_ref, w_hbm, sf_ref, res_ref, dec_ref, skip_ref, wout_hbm, out_ref,
    scaled, wbuf, woutbuf, up_send, up_recv, dn_send, dn_recv,
    sq_send, sq_recv, square, scale_ref, p_sf, p_res, p_dec, p_skip,
    fpad, halo_send, halo_recv, st_send, st_recv, local_st, gz, gated_ref, query_ref, local_y, gobuf,
    w_sem, wout_sem, up_ss, up_rs, dn_ss, dn_rs, sq_ss, sq_rs, p_ss, p_rs,
    h_ss, h_rs, st_ss, st_rs, gu_ss, gu_rs, gd_ss, gd_rs,
):
    me = lax.axis_index("ctx")
    z = lax.axis_index("ch")
    last = n_ch - 1
    width = 3 * LANES
    half = chunks * LANES
    piece_rows = rows // PIECES
    blocks = rows // SUB
    dev_ch = sf_ref.shape[2]
    is_end = (z == 0) | (z == last)
    is_mid = (z > 0) & (z < last)

    def weight_copies(index):
        start = pl.multiple_of(index * LANES, LANES)
        return [
            pltpu.make_async_copy(
                w_hbm.at[s, :, pl.ds(start, LANES)],
                wbuf.at[index, :, pl.ds(s * LANES, LANES)],
                w_sem.at[index, s],
            )
            for s in range(3)
        ]

    def start_weights(j, _):
        for copy in weight_copies(chunks + j):
            copy.start()
        for copy in weight_copies(j):
            copy.start()
        return 0

    lax.fori_loop(0, chunks, start_weights, 0)
    wout_copy = pltpu.make_async_copy(wout_hbm, woutbuf, wout_sem)
    wout_copy.start()

    barrier = pltpu.get_barrier_semaphore()
    for k in range(1, n_ch):
        pl.semaphore_signal(
            barrier, inc=1, device_id={"ch": lax.rem(z + k, n_ch)}, device_id_type=MESH
        )

    def greet(k, _):
        pl.semaphore_signal(
            barrier, inc=1, device_id={"ctx": lax.rem(me + k, n_ctx)}, device_id_type=MESH
        )
        return 0

    lax.fori_loop(1, n_ctx, greet, 0)

    wide = tok_ref[...].astype(jnp.float32)
    scaled[...] = (wide * gain_ref[...].astype(jnp.float32).reshape(1, -1)).astype(jnp.bfloat16)
    wide = wide * wide
    folded = wide[:, :LANES]
    for k in range(1, wide.shape[1] // LANES):
        folded = folded + wide[:, k * LANES : (k + 1) * LANES]
    square[...] = jnp.zeros_like(square)
    square[pl.ds(0, rows), :] = folded
    turned = jnp.sum(square[...].T, axis=0, keepdims=True)
    sq_send[...] = jnp.broadcast_to(turned, sq_send.shape)

    pl.semaphore_wait(barrier, n_ch - 1 + n_ctx - 1)

    def sq_copy(k):
        return pltpu.make_async_remote_copy(
            src_ref=sq_send, dst_ref=sq_recv.at[k - 1], send_sem=sq_ss.at[k - 1],
            recv_sem=sq_rs.at[k - 1], device_id={"ch": lax.rem(z + k, n_ch)}, device_id_type=MESH,
        )

    for k in range(1, n_ch):
        sq_copy(k).start()
    own_half = lax.rem(z, 2)
    partner = z + 1 - 2 * own_half
    p_copies = [
        pltpu.make_async_remote_copy(
            src_ref=src, dst_ref=dst.at[own_half], send_sem=p_ss.at[i], recv_sem=p_rs.at[i],
            device_id={"ch": partner}, device_id_type=MESH,
        )
        for i, (src, dst) in enumerate(
            ((sf_ref, p_sf), (res_ref, p_res), (dec_ref, p_dec), (skip_ref, p_skip))
        )
    ]
    for copy in p_copies:
        copy.start()
    p_sf[own_half] = sf_ref[...]
    p_res[own_half] = res_ref[...]
    p_dec[own_half] = dec_ref[...]
    p_skip[own_half] = skip_ref[...]

    def partial(index):
        for copy in weight_copies(index):
            copy.wait()
        return jnp.dot(scaled[...], wbuf[index], preferred_element_type=jnp.float32)

    def up_copy(j, i):
        span = pl.ds(i * piece_rows, piece_rows)
        return pltpu.make_async_remote_copy(
            src_ref=up_send.at[j, span], dst_ref=up_recv.at[j, span], send_sem=up_ss.at[j, i],
            recv_sem=up_rs.at[j, i], device_id={"ch": jnp.minimum(z + 1, last)}, device_id_type=MESH,
        )

    def dn_copy(j, i):
        span = pl.ds(i * piece_rows, piece_rows)
        return pltpu.make_async_remote_copy(
            src_ref=dn_send.at[j, span], dst_ref=dn_recv.at[j, span], send_sem=dn_ss.at[j, i],
            recv_sem=dn_rs.at[j, i], device_id={"ch": jnp.maximum(z - 1, 0)}, device_id_type=MESH,
        )

    def halo_copy(j):
        return pltpu.make_async_remote_copy(
            src_ref=halo_send.at[j], dst_ref=halo_recv.at[j], send_sem=h_ss.at[j],
            recv_sem=h_rs.at[j], device_id={"ctx": jnp.minimum(me + 1, n_ctx - 1)}, device_id_type=MESH,
        )

    def state_copy(j, k):
        return pltpu.make_async_remote_copy(
            src_ref=st_send.at[j], dst_ref=st_recv.at[j, k - 1], send_sem=st_ss.at[j],
            recv_sem=st_rs.at[j], device_id={"ctx": lax.rem(me + k, n_ctx)}, device_id_type=MESH,
        )

    def gu_copy(j):
        piece = gobuf.at[:, pl.ds(pl.multiple_of(j * LANES, LANES), LANES)]
        return pltpu.make_async_remote_copy(
            src_ref=piece, dst_ref=piece, send_sem=gu_ss.at[j],
            recv_sem=gu_rs.at[j], device_id={"ch": jnp.minimum(z + 1, last)}, device_id_type=MESH,
        )

    def gd_copy(j):
        piece = gobuf.at[:, pl.ds(pl.multiple_of(half + j * LANES, LANES), LANES)]
        return pltpu.make_async_remote_copy(
            src_ref=piece, dst_ref=piece, send_sem=gd_ss.at[j],
            recv_sem=gd_rs.at[j], device_id={"ch": jnp.maximum(z - 1, 0)}, device_id_type=MESH,
        )

    def finish_scale():
        total = sq_send[...]
        for k in range(1, n_ch):
            total = total + sq_recv[k - 1]
        mean_sq = jnp.broadcast_to(total[0:1] * (1.0 / D), (LANES, total.shape[1])).T
        scale_ref[...] = lax.rsqrt(mean_sq + 1e-06)[:rows]

    def stage_a(j, proj):
        scale = scale_ref[...]
        for s in range(3):
            feats = (proj[:, s * LANES : (s + 1) * LANES] * scale).astype(jnp.bfloat16)
            fpad[j, s, pl.ds(HALO, rows), :] = feats.astype(jnp.float32)
            halo_send[j, s] = feats[rows - HALO :]

        @pl.when(me < n_ctx - 1)
        def _():
            halo_copy(j).start()

    def lane_of(j):
        per = dev_ch // LANES
        return j // per, pl.ds(pl.multiple_of(lax.rem(j, per) * LANES, LANES), LANES)

    def stage_b(j):
        side, lanes = lane_of(j)

        @pl.when(me > 0)
        def _():
            halo_copy(j).wait_recv()
            for s in range(3):
                fpad[j, s, pl.ds(0, HALO), :] = halo_recv[j, s].astype(jnp.float32)

        @pl.when(me == 0)
        def _():
            for s in range(3):
                fpad[j, s, pl.ds(0, HALO), :] = jnp.zeros((HALO, LANES), jnp.float32)

        def featurized(s):
            total = p_sf[side, 0, pl.ds(s, 1), lanes] * fpad[j, s, pl.ds(HALO, rows), :]
            for lag in range(1, SHORT):
                tap = p_sf[side, lag, pl.ds(s, 1), lanes]
                total = total + tap * fpad[j, s, pl.ds(HALO - lag, rows), :]
            return total

        query_ref[j] = featurized(0)
        gated = (featurized(1) * featurized(2)).astype(jnp.bfloat16).astype(jnp.float32)
        gated_ref[j] = gated
        for b in range(blocks):
            gz[b, pl.ds(SUB, SUB), :] = gated[b * SUB : (b + 1) * SUB]
        decay = p_dec[side, :, lanes]
        weight = p_res[side, :, lanes] * jnp.sqrt(2.0 * decay)
        lag_rows = lax.broadcasted_iota(jnp.int32, (SUB, LANES), 0).astype(jnp.float32)
        taps = jnp.zeros((SUB, LANES), jnp.float32)
        for r in range(ORDER):
            taps = taps + weight[r : r + 1] * jnp.exp(-decay[r : r + 1] * lag_rows)
        falls = [jnp.exp(decay * (-float(SUB - 1 - u))) for u in range(SUB)]
        jump = jnp.exp(decay * (-float(SUB)))

        def block(b, state):
            local_st[j, b] = state
            total = taps[0:1] * gz[b, pl.ds(SUB, SUB), :]
            for k in range(1, SUB):
                total = total + taps[k : k + 1] * gz[b, pl.ds(SUB - k, SUB), :]
            local_y[j, b] = total
            state = state * jump
            for u in range(SUB):
                state = state + falls[u] * gz[b, pl.ds(SUB + u, 1), :]
            return state

        state = lax.fori_loop(0, blocks, block, jnp.zeros((ORDER, LANES), jnp.float32))
        st_send[j // 2, lax.rem(j, 2)] = state

        def send(k, _):
            state_copy(j // 2, k).start()
            return 0

        @pl.when(lax.rem(j, 2) == 1)
        def _():
            lax.fori_loop(1, n_ctx, send, 0)

    def stage_c(j):
        side, lanes = lane_of(j)
        pair = j // 2

        @pl.when(lax.rem(j, 2) == 0)
        def _():
            pltpu.make_async_copy(st_recv.at[pair], st_recv.at[pair], st_rs.at[pair]).wait()

        decay = p_dec[side, :, lanes]
        weight = p_res[side, :, lanes] * jnp.sqrt(2.0 * decay)

        def gather(k, state):
            far = jnp.full((ORDER, LANES), (k - 1) * rows, jnp.int32).astype(jnp.float32)
            term = jnp.exp(-decay * far) * st_recv[pair, k - 1, lax.rem(j, 2)]
            return state + jnp.where(jnp.full((ORDER, LANES), k, jnp.int32) <= me, term, 0.0)

        incoming = lax.fori_loop(1, n_ctx, gather, jnp.zeros((ORDER, LANES), jnp.float32))
        lag_rows = lax.broadcasted_iota(jnp.int32, (SUB, LANES), 0).astype(jnp.float32) + 1.0
        tables = [
            weight[r : r + 1] * jnp.exp(-decay[r : r + 1] * lag_rows) for r in range(ORDER)
        ]
        jump = jnp.exp(decay * (-float(SUB)))
        skip = p_skip[side, :, lanes]
        start = pl.multiple_of(jnp.where(z == 0, 0, half) + j * LANES, LANES)
        for b in range(blocks):
            state = local_st[j, b] + incoming
            total = local_y[j, b]
            for r in range(ORDER):
                total = total + tables[r] * state[r : r + 1]
            conv = total.astype(jnp.bfloat16).astype(jnp.float32)
            span = pl.ds(b * SUB, SUB)
            mixed = query_ref[j, span, :] * (conv + skip * gated_ref[j, span, :])
            gobuf[span, pl.ds(start, LANES)] = mixed.astype(jnp.bfloat16)
            incoming = incoming * jump

        @pl.when(z == 0)
        def _():
            gu_copy(j).start()

        @pl.when(z == last)
        def _():
            gd_copy(j).start()

    def lead_up(j, _):
        up_send[j] = partial(chunks + j).astype(jnp.bfloat16)
        for i in range(PIECES):
            up_copy(j, i).start()
        return 0

    def lead_dn(j, _):
        dn_send[j] = partial(j).astype(jnp.bfloat16)
        for i in range(PIECES):
            dn_copy(j, i).start()
        return 0

    @pl.when(z == 0)
    def _():
        lax.fori_loop(0, LEAD, lead_up, 0)

    @pl.when(z == last)
    def _():
        lax.fori_loop(0, LEAD, lead_dn, 0)

    gz[...] = jnp.zeros_like(gz)
    def settle():
        for k in range(1, n_ch):
            sq_copy(k).wait()
        for copy in p_copies:
            copy.wait()

    @pl.when(is_end)
    def _():
        settle()
        finish_scale()

    def step(s, _):
        cu = s + 1 - z
        cd = s + 1 - (last - z)
        fin = s

        @pl.when((z == 0) & (s + LEAD < chunks))
        def _():
            lead_up(s + LEAD, 0)

        @pl.when((z == last) & (s + LEAD < chunks))
        def _():
            lead_dn(s + LEAD, 0)

        @pl.when(is_mid & (cu >= 0) & (cu < chunks))
        def _():
            total = partial(chunks + cu)
            for i in range(PIECES):
                span = pl.ds(i * piece_rows, piece_rows)
                up_copy(cu, i).wait_recv()
                mine = total[i * piece_rows : (i + 1) * piece_rows]
                theirs = up_recv[cu, span, :].astype(jnp.float32)
                up_send[cu, span, :] = (mine + theirs).astype(jnp.bfloat16)
                up_copy(cu, i).start()

        @pl.when(is_mid & (cd >= 0) & (cd < chunks))
        def _():
            total = partial(cd)
            for i in range(PIECES):
                span = pl.ds(i * piece_rows, piece_rows)
                dn_copy(cd, i).wait_recv()
                mine = total[i * piece_rows : (i + 1) * piece_rows]
                theirs = dn_recv[cd, span, :].astype(jnp.float32)
                dn_send[cd, span, :] = (mine + theirs).astype(jnp.bfloat16)
                dn_copy(cd, i).start()

        @pl.when(is_end & (fin >= 5) & (fin < chunks + 5))
        def _():
            stage_c(fin - 5)

        @pl.when(is_end & (fin >= 2) & (fin < chunks + 2))
        def _():
            stage_b(fin - 2)

        @pl.when((z == 0) & (fin >= 0) & (fin < chunks))
        def _():
            total = partial(fin)
            for i in range(PIECES):
                dn_copy(fin, i).wait_recv()
            stage_a(fin, total + dn_recv[fin].astype(jnp.float32))

        @pl.when((z == last) & (fin >= 0) & (fin < chunks))
        def _():
            total = partial(chunks + fin)
            for i in range(PIECES):
                up_copy(fin, i).wait_recv()
            stage_a(fin, total + up_recv[fin].astype(jnp.float32))

        fu = s - chunks + 1 - 2 * z
        fd = s - chunks + 1 - 2 * (last - z)

        @pl.when((z > 0) & (z < last) & (fu >= 0) & (fu < chunks))
        def _():
            gu_copy(fu).wait_recv()
            gu_copy(fu).start()

        @pl.when((z > 0) & (z < last) & (fd >= 0) & (fd < chunks))
        def _():
            gd_copy(fd).wait_recv()
            gd_copy(fd).start()

        return 0

    lax.fori_loop(0, 2 * chunks - 1 + 2 * (last - 1), step, 0)

    @pl.when(is_mid)
    def _():
        settle()

    wout_copy.wait()

    def finish(j, _):
        @pl.when(z < last)
        def _():
            for i in range(PIECES):
                up_copy(j, i).wait_send()
            gu_copy(j).wait_send()

        @pl.when(z > 0)
        def _():
            for i in range(PIECES):
                dn_copy(j, i).wait_send()
            gd_copy(j).wait_send()

        @pl.when(z == last)
        def _():
            gu_copy(j).wait_recv()

        @pl.when(z == 0)
        def _():
            gd_copy(j).wait_recv()

        @pl.when(is_end & (me < n_ctx - 1))
        def _():
            halo_copy(j).wait_send()

        @pl.when(is_end & (j < chunks // 2))
        def _():
            pltpu.make_async_copy(st_recv.at[j], st_recv.at[j], st_ss.at[j]).wait()

        return 0

    lax.fori_loop(0, chunks, finish, 0)

    tile = 256

    def project(t, _):
        cols = pl.ds(pl.multiple_of(t * tile, tile), tile)
        out_ref[:, cols] = jnp.dot(
            gobuf[...], woutbuf[:, cols], preferred_element_type=jnp.float32
        ).astype(jnp.bfloat16)
        return 0

    lax.fori_loop(0, out_ref.shape[1] // tile, project, 0)


def local(tokens_in, norm_gain, w_qkv, short_filter, residue, decay_rate, skip_bias, w_out):
    rows, feat = tokens_in.shape
    slab = w_qkv.shape[2]
    dev_ch = short_filter.shape[2]
    n_ctx = lax.axis_size("ctx")
    n_ch = lax.axis_size("ch")
    chunks = slab // 2 // LANES
    width = 3 * LANES
    padded = -(-rows // LANES) * LANES
    blocks = rows // SUB
    vmem = pl.BlockSpec(memory_space=pltpu.VMEM)
    hbm = pl.BlockSpec(memory_space=pl.ANY)
    bf, f32 = jnp.bfloat16, jnp.float32
    dma = pltpu.SemaphoreType.DMA
    V = pltpu.VMEM
    return pl.pallas_call(
        functools.partial(kernel, n_ctx, n_ch, rows, chunks),
        out_shape=jax.ShapeDtypeStruct((rows, w_out.shape[1]), bf),
        in_specs=[vmem, vmem, hbm, vmem, vmem, vmem, vmem, hbm],
        out_specs=vmem,
        scratch_shapes=[
            V((rows, feat), bf), V((2 * chunks, feat, width), bf), V(w_out.shape, bf),
            V((chunks, rows, width), bf), V((chunks, rows, width), bf),
            V((chunks, rows, width), bf), V((chunks, rows, width), bf),
            V((8, padded), f32), V((n_ch - 1, 8, padded), f32), V((padded, LANES), f32),
            V((rows, LANES), f32),
            V((2, SHORT, 3, dev_ch), f32), V((2, ORDER, dev_ch), f32), V((2, ORDER, dev_ch), f32),
            V((2, 1, dev_ch), f32),
            V((chunks, 3, HALO + rows, LANES), f32),
            V((chunks, 3, HALO, LANES), bf), V((chunks, 3, HALO, LANES), bf),
            V((chunks // 2, 2, ORDER, LANES), f32), V((chunks // 2, n_ctx - 1, 2, ORDER, LANES), f32),
            V((chunks, blocks, ORDER, LANES), f32), V((blocks, 2 * SUB, LANES), f32),
            V((chunks, rows, LANES), f32), V((chunks, rows, LANES), f32),
            V((chunks, blocks, SUB, LANES), f32), V((rows, slab), bf),
            dma((2 * chunks, 3)), dma, dma((chunks, PIECES)), dma((chunks, PIECES)),
            dma((chunks, PIECES)), dma((chunks, PIECES)),
            dma((n_ch - 1,)), dma((n_ch - 1,)), dma((4,)), dma((4,)),
            dma((chunks,)), dma((chunks,)), dma((chunks // 2,)), dma((chunks // 2,)),
            dma((chunks,)), dma((chunks,)), dma((chunks,)), dma((chunks,)),
        ],
        compiler_params=pltpu.CompilerParams(
            collective_id=0, has_side_effects=True, vmem_limit_bytes=56 * 2**20
        ),
        name="hyena",
    )(
        tokens_in, norm_gain, jnp.transpose(w_qkv, (1, 0, 2)), short_filter,
        residue.T, decay_rate.T, skip_bias.reshape(1, dev_ch), w_out,
    )


def solution(mesh):
    return jax.shard_map(
        local,
        mesh=mesh,
        in_specs=(
            P("ctx", "ch"),
            P("ch"),
            P("ch", None, None),
            P(None, None, "ch"),
            P("ch", None),
            P("ch", None),
            P("ch"),
            P(None, "ch"),
        ),
        out_specs=P("ctx", "ch"),
        check_vma=False,
    )
```
